32 devices in a mesh: row: 8 (over y, x, core), col: 4 (over z).
Axes of the slice: x: 2, y: 2, z: 4, core: 2. Of those that a mesh axis runs over, the one named last changes fastest.
Arguments:
- features: bfloat16 [4096, 1024], P(('row', 'col')), may hold values from -6 to 6
- node_valid: int32 [32, 128], P(('row', 'col')), may hold values 0 or 1
- self_mask: int32 [32, 128, 128], P(('row', 'col')), may hold values 0 or 1
- pair_blocks: int32 [8, 4, 8, 2], P('row', 'col'), may hold values from 0 to 31, as said below
- pair_count: int32 [8, 4], P('row', 'col'), may hold values from 0 to 8, as said below
- pair_masks: int32 [8, 4, 8, 128, 128], P('row', 'col'), may hold values 0 or 1
- weight_src: bfloat16 [1024, 1024], replicated, may hold values from -0.1875 to 0.1875
- weight_tgt: bfloat16 [1024, 1024], replicated, may hold values from -0.1875 to 0.1875
- attn: float32 [4, 256], replicated
- bias: float32 [1024], replicated, may hold values from -6 to 6
Outputs:
- attended: bfloat16 [4096, 1024], P(('row', 'col'))
The draws below stay inside these ranges and needn't reach their ends.
Inputs may be any that keep to these rules, and one draw needn't show every extreme that they name: `pair_blocks`: cell (r, c) lists in each slot a pair (i, j) of different blocks: i is held by a device of grid row r and j by a device of grid column c, block b being held by device b // 1 counted row by row. No unordered pair stands in two live slots. Slots from pair_count on are not used. Some cell has all 8 slots live.
All inputs are finite; a program needn't handle non-finite values. No bound on the sum of `node_valid` or of `self_mask` or of `pair_masks` on one device may be relied on, other than what follows from the above.
Results may differ from the reference program's by a relative error of at most 0.012.
The reference program's roundings to bfloat16 on the way (of `source`, `target` and `weights`) count: a program that leaves them out, or rounds other values in their place, can miss the bound.
Values may be sent and summed in bfloat16 or wider, within the bound.
A program may use at most 128 MiB of HBM per device.

```python
import math
import jax
import jax.numpy as jnp
from jax import lax

D = 1024
H = 4
HS = 256
BS = 128
CELL_CAPACITY = 8
BLK = 1
NB = 32
NODES = 4096
N_ROW = 8
N_COL = 4


def pair_table(key):
    starting_index = jax.random.fold_in(key, 4099)
    selection_seed, tally_seed, clumping_seed = jax.random.split(starting_index, 3)
    span_row = N_COL * BLK
    span_col = N_ROW * BLK
    total = span_row * span_col
    grid_rows = jnp.arange(N_ROW, dtype=jnp.int32).reshape(N_ROW, 1, 1, 1)
    grid_cols = jnp.arange(N_COL, dtype=jnp.int32).reshape(1, N_COL, 1, 1)
    row_slot = jnp.arange(span_row, dtype=jnp.int32).reshape(1, 1, span_row, 1)
    col_slot = jnp.arange(span_col, dtype=jnp.int32).reshape(1, 1, 1, span_col)
    shape = (N_ROW, N_COL, span_row, span_col)
    first = jnp.broadcast_to(grid_rows * span_row + row_slot, shape).reshape(N_ROW, N_COL, total)
    second = jnp.broadcast_to((col_slot // BLK * N_COL + grid_cols) * BLK + col_slot % BLK, shape).reshape(N_ROW, N_COL, total)
    allowed = (first != second) & ((first < second) != ((first + second) % 2 == 1))
    noise = jax.random.randint(selection_seed, (N_ROW, N_COL, total), 0, 16384, dtype=jnp.int32)
    ranking = noise * total + jnp.arange(total, dtype=jnp.int32) + allowed.astype(jnp.int32) * (1 << 30)
    ranked, picked = lax.top_k(ranking, CELL_CAPACITY)
    first_pick = jnp.take_along_axis(first, picked, axis=2)
    second_pick = jnp.take_along_axis(second, picked, axis=2)
    listed = jnp.stack([first_pick, second_pick], axis=-1).astype(jnp.int32)
    room = jnp.sum(allowed.astype(jnp.int32), axis=2)
    couple_tallies = jax.random.randint(tally_seed, (N_ROW, N_COL), 0, 5, dtype=jnp.int32)
    clustered_couples = jax.random.randint(clumping_seed, (N_ROW, N_COL), 0, 8, dtype=jnp.int32) == 0
    couple_tallies = jnp.where(clustered_couples, CELL_CAPACITY, couple_tallies)
    couple_tallies = couple_tallies.at[0, 0].set(CELL_CAPACITY)
    couple_tallies = jnp.minimum(couple_tallies, room).astype(jnp.int32)
    return (listed, couple_tallies)


def draw_pair_blocks(key, part):
    listed, couple_tallies = pair_table(key)
    return listed


def draw_pair_count(key, part):
    listed, couple_tallies = pair_table(key)
    return couple_tallies


def draw_attn(key, part):
    values = jax.random.normal(jax.random.fold_in(key, 11), (H, HS), jnp.float32) * (2.0 / math.sqrt(HS))
    return values


def place_ends(values, key, smallest, high):
    index_at = [jax.random.randint(jax.random.fold_in(key, axis), (), 0, length) for axis, length in enumerate(values.shape)]
    longest = values.shape.index(max(values.shape))
    beside = index_at[:longest] + [(index_at[longest] + 1) % values.shape[longest]] + index_at[longest + 1:]
    return values.at[tuple(index_at)].set(smallest).at[tuple(beside)].set(high)


def level_of(stream_key, extent, cuts, low, largest):
    def one(axis_at, blocks):
        heights = jax.random.uniform(jax.random.fold_in(jax.random.fold_in(stream_key, 6), axis_at), (blocks,), jnp.float32, low / len(cuts), largest / len(cuts))
        return jnp.repeat(jnp.exp(heights), extent[axis_at] // blocks).reshape((-1,) + (1,) * (len(extent) - axis_at - 1))

    factor_of = one(*cuts[0])
    for cut in cuts[1:]:
        factor_of = factor_of * one(*cut)
    return factor_of


def centred(own_key, shape, scale, most, cuts=(), kind=jnp.bfloat16):
    values = jax.random.normal(own_key, shape, jnp.float32) * scale
    if len(cuts) > 0:
        values = level_of(own_key, shape, cuts, -0.22, 0.18) * values
    return jnp.clip(values, min=-most, max=most).astype(kind)


def setup_inputs(seed: int = 0) -> dict:
    key_of = jax.random.split(jax.random.key(seed), 11)
    return {
        "features": centred(key_of[0], (NODES, D), 1.0, 6.0, ((0, 32),)),
        "node_valid": place_ends((jax.random.randint(key_of[1], (NB, BS), 0, 8) < 7).astype(jnp.int32), jax.random.fold_in(key_of[1], 1), 0, 1),
        "self_mask": place_ends((jax.random.randint(key_of[2], (NB, BS, BS), 0, 8) < 1).astype(jnp.int32), jax.random.fold_in(key_of[2], 1), 0, 1),
        "pair_blocks": draw_pair_blocks(jax.random.fold_in(key_of[10], 71), 0),
        "pair_count": draw_pair_count(jax.random.fold_in(key_of[10], 71), 0),
        "pair_masks": place_ends((jax.random.randint(key_of[5], (N_ROW, N_COL, CELL_CAPACITY, BS, BS), 0, 8) < 1).astype(jnp.int32), jax.random.fold_in(key_of[5], 1), 0, 1),
        "weight_src": centred(key_of[6], (D, D), D ** -0.5, 0.1875),
        "weight_tgt": centred(key_of[7], (D, D), D ** -0.5, 0.1875),
        "attn": draw_attn(jax.random.fold_in(key_of[10], 71), 0),
        "bias": centred(key_of[9], (D,), 1.0, 6.0, (), jnp.float32),
    }


FLOOR = -1.0e30


def score_block(target, source, attn):
    heads = attn.shape[0]
    head_width = attn.shape[1]
    target_heads = target.reshape(target.shape[0], heads, head_width)
    source_heads = source.reshape(source.shape[0], heads, head_width)
    planes = []
    for head in range(heads):
        mixed = target_heads[:, head, :].astype(jnp.float32)[:, None, :] + source_heads[:, head, :].astype(jnp.float32)[None, :, :]
        planes.append(jnp.sum(jax.nn.leaky_relu(mixed, 0.2) * attn[head], axis=-1))
    return jnp.stack(planes)


def weigh(weights, source, heads):
    nodes = source.shape[0]
    source_heads = source.reshape(nodes, heads, source.shape[1] // heads).astype(jnp.float32)
    rounded = weights.astype(jnp.bfloat16).astype(jnp.float32)
    mixed = jnp.einsum("hts,shd->thd", rounded, source_heads, precision=lax.Precision.HIGHEST)
    return mixed.reshape(weights.shape[1], source.shape[1])


def to_wire(value):
    return lax.optimization_barrier(value.astype(jnp.bfloat16)).astype(jnp.float32)


def reference(features, node_valid, self_mask, pair_blocks, pair_count, pair_masks, weight_src, weight_tgt, attn, bias):
    blocks = node_valid.shape[0]
    block_size = node_valid.shape[1]
    width = features.shape[1]
    heads = attn.shape[0]
    head_width = attn.shape[1]
    source_all = jnp.dot(features, weight_src, preferred_element_type=jnp.float32).astype(jnp.bfloat16).reshape(blocks, block_size, width)
    target_all = jnp.dot(features, weight_tgt, preferred_element_type=jnp.float32).astype(jnp.bfloat16).reshape(blocks, block_size, width)
    valid = node_valid > 0
    span_row = N_COL * BLK
    span_col = N_ROW * BLK
    flat_blocks = pair_blocks.reshape(-1, 2)
    flat_masks = pair_masks.reshape(-1, block_size, block_size)
    slot_ids = jnp.arange(CELL_CAPACITY, dtype=jnp.int32)
    live = (slot_ids[None, None, :] < pair_count[:, :, None]).reshape(-1)

    def both(item):
        first = flat_blocks[item, 0]
        second = flat_blocks[item, 1]
        adjacency = (flat_masks[item] > 0) & valid[first][:, None] & valid[second][None, :]
        forward = jnp.where(adjacency[None], score_block(target_all[first], source_all[second], attn), FLOOR)
        backward = jnp.where(adjacency.T[None], score_block(target_all[second], source_all[first], attn), FLOOR)
        return first, second, adjacency, forward, backward

    def max_pass(item, carry):
        def live_step(state):
            first, second, adjacency, forward, backward = both(item)
            return (state[0].at[first].max(jnp.max(forward, axis=-1)), state[1].at[second].max(jnp.max(backward, axis=-1)))
        return lax.cond(live[item], live_step, lambda state: state, carry)

    start_peak = jnp.full((blocks, heads, block_size), FLOOR, jnp.float32)
    row_peak, col_peak = lax.fori_loop(0, flat_blocks.shape[0], max_pass, (start_peak, start_peak))

    def cell_pass(cell, totals):
        grid_row = cell // N_COL
        grid_col = cell % N_COL

        def slot_pass(slot, parts):
            item = cell * CELL_CAPACITY + slot

            def live_step(state):
                first, second, adjacency, forward, backward = both(item)
                row_slot = first - grid_row * span_row
                col_slot = (second // BLK) // N_COL * BLK + second % BLK
                weights_fwd = jnp.where(adjacency[None], jnp.exp(forward - row_peak[first][:, :, None]), 0.0)
                weights_bwd = jnp.where(adjacency.T[None], jnp.exp(backward - col_peak[second][:, :, None]), 0.0)
                numer_fwd = weigh(weights_fwd, source_all[second], heads)
                numer_bwd = weigh(weights_bwd, source_all[first], heads)
                return (state[0].at[row_slot].add(numer_fwd), state[1].at[row_slot].add(jnp.sum(weights_fwd, axis=-1)),
                        state[2].at[col_slot].add(numer_bwd), state[3].at[col_slot].add(jnp.sum(weights_bwd, axis=-1)))
            return lax.cond(live[item], live_step, lambda state: state, parts)

        parts = (jnp.zeros((span_row, block_size, width), jnp.float32), jnp.zeros((span_row, heads, block_size), jnp.float32),
                 jnp.zeros((span_col, block_size, width), jnp.float32), jnp.zeros((span_col, heads, block_size), jnp.float32))
        parts = lax.fori_loop(0, CELL_CAPACITY, slot_pass, parts)
        row_numer = totals[0].at[grid_row].add(to_wire(parts[0]).reshape(N_COL, BLK, block_size, width))
        row_denom = totals[1].at[grid_row].add(to_wire(parts[1]).reshape(N_COL, BLK, heads, block_size))
        col_numer = totals[2].at[:, grid_col].add(to_wire(parts[2]).reshape(N_ROW, BLK, block_size, width))
        col_denom = totals[3].at[:, grid_col].add(to_wire(parts[3]).reshape(N_ROW, BLK, heads, block_size))
        return (row_numer, row_denom, col_numer, col_denom)

    totals = (jnp.zeros((N_ROW, N_COL, BLK, block_size, width), jnp.float32), jnp.zeros((N_ROW, N_COL, BLK, heads, block_size), jnp.float32),
              jnp.zeros((N_ROW, N_COL, BLK, block_size, width), jnp.float32), jnp.zeros((N_ROW, N_COL, BLK, heads, block_size), jnp.float32))
    totals = lax.fori_loop(0, N_ROW * N_COL, cell_pass, totals)
    row_numer = totals[0].reshape(blocks, block_size, width)
    row_denom = totals[1].reshape(blocks, heads, block_size)
    col_numer = totals[2].reshape(blocks, block_size, width)
    col_denom = totals[3].reshape(blocks, heads, block_size)
    identity = jnp.eye(block_size, dtype=bool)

    def finish(block):
        flags = valid[block]
        adjacency = ((self_mask[block] > 0) | identity) & flags[:, None] & flags[None, :]
        scores = jnp.where(adjacency[None], score_block(target_all[block], source_all[block], attn), FLOOR)
        top = jnp.maximum(jnp.maximum(row_peak[block], col_peak[block]), jnp.max(scores, axis=-1))
        weights = jnp.where(adjacency[None], jnp.exp(scores - top[:, :, None]), 0.0)
        own = weigh(weights, source_all[block], heads).reshape(block_size, heads, head_width)
        row_scale = jnp.exp(row_peak[block] - top)
        col_scale = jnp.exp(col_peak[block] - top)
        numer = own + row_numer[block].reshape(block_size, heads, head_width) * row_scale.T[:, :, None]
        numer = numer + col_numer[block].reshape(block_size, heads, head_width) * col_scale.T[:, :, None]
        denom = jnp.sum(weights, axis=-1) + row_denom[block] * row_scale + col_denom[block] * col_scale
        denom = denom + (1.0 - flags.astype(jnp.float32))[None, :]
        result = (numer / denom.T[:, :, None]).reshape(block_size, width) + bias[None, :]
        return result.astype(jnp.bfloat16)

    return lax.map(finish, jnp.arange(blocks, dtype=jnp.int32)).reshape(blocks * block_size, width)
```

```python
import functools

import jax
import jax.numpy as jnp
from jax import lax
from jax.experimental import pallas as pl
from jax.experimental.pallas import tpu as pltpu
from jax.sharding import PartitionSpec as P

FLOOR = -1e30


def score_block(target, source, attn):
    heads = attn.shape[0]
    head_width = attn.shape[1]
    target_heads = target.reshape(target.shape[0], heads, head_width)
    source_heads = source.reshape(source.shape[0], heads, head_width)
    planes = []
    for head in range(heads):
        mixed = (
            target_heads[:, head, :].astype(jnp.float32)[:, None, :]
            + source_heads[:, head, :].astype(jnp.float32)[None, :, :]
        )
        planes.append(jnp.sum(jax.nn.leaky_relu(mixed, 0.2) * attn[head], axis=-1))
    return jnp.stack(planes)


def weigh(weights, source, heads):
    nodes = source.shape[0]
    source_heads = source.reshape(nodes, heads, source.shape[1] // heads)
    mixed = jnp.einsum(
        "hts,shd->thd",
        weights.astype(jnp.bfloat16),
        source_heads,
        preferred_element_type=jnp.float32,
    )
    return mixed.reshape(weights.shape[1], source.shape[1])


def raise_at(table, position, values):
    current = lax.dynamic_index_in_dim(table, position, 0, keepdims=False)
    return lax.dynamic_update_index_in_dim(table, jnp.maximum(current, values), position, 0)


def add_index(table, position, values):
    current = lax.dynamic_index_in_dim(table, position, 0, keepdims=False)
    return lax.dynamic_update_index_in_dim(table, current + values, position, 0)


def add_rows(table, start, values):
    current = lax.dynamic_slice_in_dim(table, start, values.shape[0], 0)
    return lax.dynamic_update_slice_in_dim(table, current + values, start, 0)


def general_body(
    features,
    node_valid,
    self_mask,
    pair_blocks,
    pair_count,
    pair_masks,
    weight_src,
    weight_tgt,
    attn,
    bias,
):
    owned = node_valid.shape[0]
    block_size = node_valid.shape[1]
    width = features.shape[1]
    heads = attn.shape[0]
    head_width = attn.shape[1]
    row_devices = lax.axis_size("row")
    col_devices = lax.axis_size("col")
    my_row = lax.axis_index("row")
    my_col = lax.axis_index("col")
    valid_flags = node_valid.astype(jnp.bfloat16)
    source_own = jnp.dot(features, weight_src, preferred_element_type=jnp.float32).astype(
        jnp.bfloat16
    )
    target_own = jnp.dot(features, weight_tgt, preferred_element_type=jnp.float32).astype(
        jnp.bfloat16
    )
    packed = jnp.concatenate([source_own, target_own], axis=1)
    row_store, row_valid = (
        lax.all_gather(packed, "col", axis=0, tiled=True),
        lax.all_gather(valid_flags, "col", axis=0, tiled=True),
    )
    col_store, col_valid = (
        lax.all_gather(packed, "row", axis=0, tiled=True),
        lax.all_gather(valid_flags, "row", axis=0, tiled=True),
    )

    def fetch(store, flags, position):
        rows = lax.dynamic_slice_in_dim(store, position * block_size, block_size, 0)
        return (
            rows[:, :width],
            rows[:, width:],
            lax.dynamic_index_in_dim(flags, position, 0, keepdims=False),
        )

    span_row = col_devices * owned
    span_col = row_devices * owned
    live_count = pair_count[0, 0]
    row_peak = jnp.full((span_row, heads, block_size), FLOOR, jnp.float32)
    col_peak = jnp.full((span_col, heads, block_size), FLOOR, jnp.float32)
    kept = []
    for slot in range(pair_blocks.shape[2]):
        first = pair_blocks[0, 0, slot, 0]
        second = pair_blocks[0, 0, slot, 1]
        row_slot = first - my_row * span_row
        col_slot = second // owned // col_devices * owned + second % owned
        is_live = slot < live_count

        def live_scores(operand):
            row_at, col_at, pair_mask = operand
            source_first, target_first, flags_first = fetch(row_store, row_valid, row_at)
            source_second, target_second, flags_second = fetch(col_store, col_valid, col_at)
            adjacency = (pair_mask > 0) & (flags_first[:, None] > 0) & (flags_second[None, :] > 0)
            forward = jnp.where(
                adjacency[None], score_block(target_first, source_second, attn), FLOOR
            )
            backward = jnp.where(
                adjacency.T[None], score_block(target_second, source_first, attn), FLOOR
            )
            return (adjacency, forward, backward, source_first, source_second)

        def dead_scores(operand):
            adjacency = jnp.zeros((block_size, block_size), bool)
            blank = jnp.full((heads, block_size, block_size), FLOOR, jnp.float32)
            empty = jnp.zeros((block_size, width), jnp.bfloat16)
            return (adjacency, blank, blank, empty, empty)

        adjacency, forward, backward, source_first, source_second = lax.cond(
            is_live, live_scores, dead_scores, (row_slot, col_slot, pair_masks[0, 0, slot])
        )
        row_peak = raise_at(row_peak, row_slot, jnp.max(forward, axis=-1))
        col_peak = raise_at(col_peak, col_slot, jnp.max(backward, axis=-1))
        kept.append(
            (is_live, row_slot, col_slot, adjacency, forward, backward, source_first, source_second)
        )
    row_peak = lax.pmax(row_peak.astype(jnp.bfloat16), "col").astype(row_peak.dtype)
    col_peak = lax.pmax(col_peak.astype(jnp.bfloat16), "row").astype(col_peak.dtype)
    row_numer = jnp.zeros((span_row * block_size, width), jnp.float32)
    row_denom = jnp.zeros((span_row, heads, block_size), jnp.float32)
    col_numer = jnp.zeros((span_col * block_size, width), jnp.float32)
    col_denom = jnp.zeros((span_col, heads, block_size), jnp.float32)
    for (
        is_live,
        row_slot,
        col_slot,
        adjacency,
        forward,
        backward,
        source_first,
        source_second,
    ) in kept:
        peak_first = lax.dynamic_index_in_dim(row_peak, row_slot, 0, keepdims=False)
        peak_second = lax.dynamic_index_in_dim(col_peak, col_slot, 0, keepdims=False)

        def live_terms(operand):
            mask_now, fwd, bwd, src_first, src_second, top_first, top_second = operand
            weights_fwd = jnp.where(mask_now[None], jnp.exp(fwd - top_first[:, :, None]), 0.0)
            weights_bwd = jnp.where(mask_now.T[None], jnp.exp(bwd - top_second[:, :, None]), 0.0)
            return (
                weigh(weights_fwd, src_second, heads),
                weigh(weights_bwd, src_first, heads),
                jnp.sum(weights_fwd, axis=-1),
                jnp.sum(weights_bwd, axis=-1),
            )

        def dead_terms(operand):
            rows_zero = jnp.zeros((block_size, width), jnp.float32)
            sums_zero = jnp.zeros((heads, block_size), jnp.float32)
            return (rows_zero, rows_zero, sums_zero, sums_zero)

        numer_fwd, numer_bwd, denom_fwd, denom_bwd = lax.cond(
            is_live,
            live_terms,
            dead_terms,
            (adjacency, forward, backward, source_first, source_second, peak_first, peak_second),
        )
        row_numer = add_rows(row_numer, row_slot * block_size, numer_fwd)
        col_numer = add_rows(col_numer, col_slot * block_size, numer_bwd)
        row_denom = add_index(row_denom, row_slot, denom_fwd)
        col_denom = add_index(col_denom, col_slot, denom_bwd)
    row_numer, row_denom = (
        lax.psum_scatter(
            row_numer.astype(jnp.bfloat16), "col", scatter_dimension=0, tiled=True
        ).astype(jnp.float32),
        lax.psum_scatter(
            row_denom.astype(jnp.bfloat16), "col", scatter_dimension=0, tiled=True
        ).astype(jnp.float32),
    )
    col_numer, col_denom = (
        lax.psum_scatter(
            col_numer.astype(jnp.bfloat16), "row", scatter_dimension=0, tiled=True
        ).astype(jnp.float32),
        lax.psum_scatter(
            col_denom.astype(jnp.bfloat16), "row", scatter_dimension=0, tiled=True
        ).astype(jnp.float32),
    )
    own_row_peak = lax.dynamic_slice_in_dim(row_peak, my_col * owned, owned, 0)
    own_col_peak = lax.dynamic_slice_in_dim(col_peak, my_row * owned, owned, 0)
    identity = jnp.eye(block_size, dtype=bool)
    flags = node_valid[0] > 0
    adjacency = ((self_mask[0] > 0) | identity) & flags[:, None] & flags[None, :]
    scores = jnp.where(adjacency[None], score_block(target_own, source_own, attn), FLOOR)
    top = jnp.maximum(jnp.maximum(own_row_peak[0], own_col_peak[0]), jnp.max(scores, axis=-1))
    weights = jnp.where(adjacency[None], jnp.exp(scores - top[:, :, None]), 0.0)
    own = weigh(weights, source_own, heads).reshape(block_size, heads, head_width)
    row_scale = jnp.exp(own_row_peak[0] - top)
    col_scale = jnp.exp(own_col_peak[0] - top)
    numer = own + row_numer.reshape(block_size, heads, head_width) * row_scale.T[:, :, None]
    numer = numer + col_numer.reshape(block_size, heads, head_width) * col_scale.T[:, :, None]
    denom = jnp.sum(weights, axis=-1) + row_denom[0] * row_scale + col_denom[0] * col_scale
    denom = denom + (1.0 - flags.astype(jnp.float32))[None, :]
    result = (numer / denom.T[:, :, None]).reshape(block_size, width) + bias[None, :]
    results = result.astype(jnp.bfloat16)
    return results


NT = (((1,), (1,)), ((), ()))


def attend_kernel(rows, cols, table, source, target, masks, flags, attn_main, attn_scaled, attn_rows,
                  bias, out, top, total, numer, target_term, source_term):
    blocks, nodes, width = source.shape
    slice_rows = target.shape[1]
    slots = (masks.shape[2] - 1) // 2
    half = attn_main.shape[0] // 2

    def project(block_source, lhs):
        both = lax.dot_general(lhs, block_source, NT, preferred_element_type=jnp.float32)
        return both[:half] + both[half:]

    def scores_of(block_target, block_source):
        lhs = attn_scaled[...]
        tiles = []
        index = lax.broadcasted_iota(jnp.int32, (half, nodes), 0)
        for base in range(0, slice_rows, half):
            tile = jnp.zeros((half, nodes), jnp.float32)
            for step in range(0, half, 2):
                at = base + step
                mixed = jnp.concatenate(
                    [
                        jnp.minimum(block_target[at : at + 1, :], block_source),
                        jnp.minimum(block_target[at + 1 : at + 2, :], block_source),
                    ],
                    axis=0,
                )
                both = project(mixed, lhs)
                tile = jnp.where(index == step, both[:, :nodes], tile)
                tile = jnp.where(index == step + 1, both[:, nodes:], tile)
            tiles.append(tile)
        return jnp.concatenate(tiles, axis=0)

    def item(block, other, mask, first):
        block_source = source[other]
        scores = scores_of(target[block], block_source)
        scores = scores + target_term[block] + source_term[other][:1, :]
        keep = mask.astype(jnp.float32) * flags[other].astype(jnp.float32) > 0
        scores = jnp.where(keep, scores, FLOOR)
        peak = jnp.max(scores, axis=1, keepdims=True)
        if first:
            now = jnp.broadcast_to(peak, scores.shape)
        else:
            before = top[block]
            now = jnp.maximum(before, peak)
        weights = jnp.where(keep, jnp.exp(scores - now), 0.0)
        sums = jnp.broadcast_to(jnp.sum(weights, axis=1, keepdims=True), scores.shape)
        mixed = jnp.dot(weights.astype(jnp.bfloat16), block_source, preferred_element_type=jnp.float32)
        if not first:
            scale = jnp.exp(before - now)
            sums = sums + total[block] * scale
            mixed = mixed + numer[block] * scale[:, :1]
        top[block] = now
        total[block] = sums
        numer[block] = mixed

    def prepare(block, carry):
        block_target = target[block].astype(jnp.float32)
        source_term[block] = project(source[block], attn_main[...])
        term = jnp.sum(block_target * attn_rows[...], axis=1, keepdims=True)
        target_term[block] = jnp.broadcast_to(term, (slice_rows, nodes))
        item(block, block, masks[block % cols, block // cols, 2 * slots], True)
        return carry

    lax.fori_loop(0, blocks, prepare, 0)

    def cell(index, carry):
        grid_row, grid_col = index // cols, index % cols

        def pair(slot, inner):
            first = table[index, 2 * slot]
            second = table[index, 2 * slot + 1]
            item(first, second, masks[grid_col, grid_row, slot], False)
            item(second, first, masks[grid_col, grid_row, slots + slot], False)
            return inner

        return lax.fori_loop(0, table[index, 2 * slots], pair, carry)

    lax.fori_loop(0, rows * cols, cell, 0)

    def finish(block, carry):
        sums = total[block][:, :1]
        sums = jnp.where(sums > 0, sums, 1.0)
        out[block] = (numer[block] / sums + bias[...]).astype(out.dtype)
        return carry

    lax.fori_loop(0, blocks, finish, 0)


def split_pair(values, half):
    main = values.astype(jnp.bfloat16)
    rest = (values - main.astype(jnp.float32)).astype(jnp.bfloat16)
    shape = (half, values.shape[-1])
    return jnp.concatenate([jnp.broadcast_to(main, shape), jnp.broadcast_to(rest, shape)], axis=0)


def sliced_body(features, node_valid, self_mask, pair_blocks, pair_count, pair_masks,
                weight_src, weight_tgt, attn, bias):
    nodes = node_valid.shape[1]
    width = features.shape[1]
    heads, head_width = attn.shape
    rows = lax.axis_size("row")
    cols = lax.axis_size("col")
    my_col = lax.axis_index("col")
    blocks = rows * cols
    part = nodes // rows
    slots = pair_blocks.shape[2]

    def by_head(values):
        return values.astype(jnp.bfloat16).reshape(nodes, heads, head_width).transpose(1, 0, 2)

    source_own = by_head(jnp.dot(features, weight_src, preferred_element_type=jnp.float32))
    target_own = by_head(-jnp.dot(features, weight_tgt, preferred_element_type=jnp.float32))
    packed = lax.all_to_all(jnp.concatenate([source_own, target_own], axis=2), "col", 0, 0, tiled=True)
    source_all = lax.all_gather(packed[:, :, :head_width], "row", axis=0, tiled=True)
    target_row = packed[:, :, head_width:].reshape(cols, rows, part, head_width).transpose(1, 0, 2, 3)
    target_all = lax.all_to_all(target_row, "row", 0, 0, tiled=True).reshape(blocks, part, head_width)

    pair_mask = (pair_masks[0, 0] > 0).astype(jnp.bfloat16)
    own_mask = ((self_mask > 0) | jnp.eye(nodes, dtype=bool)[None]).astype(jnp.bfloat16)
    stacked = jnp.concatenate([pair_mask, pair_mask.transpose(0, 2, 1), own_mask], axis=0)
    stacked = stacked.reshape(-1, rows, part, nodes).transpose(1, 0, 2, 3)
    stacked = lax.all_to_all(stacked, "row", 0, 0, tiled=True)
    masks = lax.all_gather(stacked, "col", axis=0, tiled=False)

    small = jnp.concatenate(
        [node_valid.reshape(1, -1), pair_blocks.reshape(1, -1), pair_count.reshape(1, 1)], axis=1
    )
    small = lax.all_gather(small, ("row", "col"), axis=0, tiled=True)
    flags = small[:, :nodes].reshape(blocks, 1, nodes).astype(jnp.float32)
    table = small[:, nodes:]

    attn_head = lax.dynamic_slice_in_dim(attn, my_col, 1, 0)
    bias_head = lax.dynamic_slice_in_dim(bias.reshape(heads, head_width), my_col, 1, 0)
    half = 8
    vmem = pl.BlockSpec(memory_space=pltpu.VMEM)
    out = pl.pallas_call(
        functools.partial(attend_kernel, rows, cols),
        out_shape=jax.ShapeDtypeStruct((blocks, part, head_width), jnp.bfloat16),
        in_specs=[pl.BlockSpec(memory_space=pltpu.SMEM)] + [vmem] * 8,
        out_specs=vmem,
        scratch_shapes=[
            pltpu.VMEM((blocks, part, nodes), jnp.float32),
            pltpu.VMEM((blocks, part, nodes), jnp.float32),
            pltpu.VMEM((blocks, part, head_width), jnp.float32),
            pltpu.VMEM((blocks, part, nodes), jnp.float32),
            pltpu.VMEM((blocks, half, nodes), jnp.float32),
        ],
        compiler_params=pltpu.CompilerParams(vmem_limit_bytes=48 * 2**20),
    )(
        table,
        source_all,
        target_all,
        masks,
        flags,
        split_pair(attn_head, half),
        split_pair(-0.8 * attn_head, half),
        -0.2 * attn_head,
        bias_head,
    )
    out = out.reshape(rows, cols, part, head_width)
    out = lax.all_to_all(out, "row", 0, 0, tiled=True)
    out = lax.all_to_all(out.transpose(1, 0, 2, 3), "col", 0, 0, tiled=True)
    out = out.reshape(heads, nodes, head_width).transpose(1, 0, 2).reshape(nodes, width)
    blank = jnp.broadcast_to(bias[None, :], (nodes, width)).astype(jnp.bfloat16)
    return jnp.where(node_valid.reshape(nodes, 1) > 0, out, blank)


def pick_body(mesh, features, node_valid, *rest):
    heads = rest[-2].shape[0]
    rows, cols = mesh.shape["row"], mesh.shape["col"]
    even = node_valid.shape[0] == 1 and cols == heads and node_valid.shape[1] % (rows * 16) == 0
    return (sliced_body if even else general_body)(features, node_valid, *rest)


def solution(mesh):
    return jax.shard_map(
        functools.partial(pick_body, mesh),
        mesh=mesh,
        in_specs=(
            P(("row", "col"), None),
            P(("row", "col"), None),
            P(("row", "col"), None, None),
            P("row", "col", None, None),
            P("row", "col"),
            P("row", "col", None, None, None),
            P(),
            P(),
            P(),
            P(),
        ),
        out_specs=P(("row", "col"), None),
        check_vma=False,
    )
```
